32 devices in a mesh: lon: 8 (over y, x, core), lat: 4 (over z).
Axes of the slice: x: 2, y: 2, z: 4, core: 2. Of those that a mesh axis runs over, the one named last changes fastest.
Arguments:
- thermal_anomaly: float32 [12, 128, 3072], P(None, 'lat', 'lon'), may hold values from -6 to 6
- saltiness_anomaly: float32 [12, 128, 3072], P(None, 'lat', 'lon'), may hold values from -6 to 6
- zonal_current: float32 [12, 128, 3072], P(None, 'lat', 'lon'), may hold values from -1.8 to 1.8
- meridional_current: float32 [12, 128, 3072], P(None, 'lat', 'lon'), may hold values from -1.8 to 1.8
- free_elevation: float32 [128, 3072], P('lat', 'lon'), may hold values from -1.8 to 1.8
- zonal_traction: float32 [128, 3072], P('lat', 'lon'), may hold values from -6 to 6
- meridional_traction: float32 [128, 3072], P('lat', 'lon'), may hold values from -6 to 6
- water_indicator: int32 [128, 3072], P('lat', 'lon'), may hold values 0 or 1
- bottom_layer_index: int32 [128, 3072], P('lat', 'lon'), may hold values from 1 to 12
Outputs:
- temperature_next: float32 [12, 128, 3072], P(None, 'lat', 'lon')
- salinity_next: float32 [12, 128, 3072], P(None, 'lat', 'lon')
- u_next: float32 [12, 128, 3072], P(None, 'lat', 'lon')
- v_next: float32 [12, 128, 3072], P(None, 'lat', 'lon')
- height_next: float32 [128, 3072], P('lat', 'lon')
- transport_x: float32 [128, 3072], P('lat', 'lon')
- transport_y: float32 [128, 3072], P('lat', 'lon')
The draws below stay inside these ranges and needn't reach their ends.
All inputs are finite; a program needn't handle non-finite values. No bound on the sum of `water_indicator` on one device may be relied on, other than what follows from the above.
Results may differ from the reference program's by a relative error of at most 0.00002.
Values sent between devices are 32-bit elements; how exact they have to be, the bound alone decides.
A program may use at most 64 MiB of HBM per device.

```python
import jax
import jax.numpy as jnp

VERTICAL_LAYERS = 12
NSUB = 4
MERIDIAN_CELLS = 128
PARALLEL_CELLS = 3072


def set_ends(drawn, own_key, smallest, top_value):
    place = [jax.random.randint(jax.random.fold_in(own_key, axis), (), 0, length) for axis, length in enumerate(drawn.shape)]
    longest = drawn.shape.index(max(drawn.shape))
    beside = place[:longest] + [(place[longest] + 1) % drawn.shape[longest]] + place[longest + 1:]
    return drawn.at[tuple(place)].set(smallest).at[tuple(beside)].set(top_value)


def steps_of(rng, dims, shards, least, largest):
    gain = 1.0
    for axis_at, parts in shards:
        steps = jax.random.uniform(jax.random.fold_in(jax.random.fold_in(rng, 6), axis_at), (parts,), jnp.float32, least / len(shards), largest / len(shards))
        gain = gain * jnp.repeat(jnp.exp(steps), dims[axis_at] // parts).reshape((-1,) + (1,) * (len(dims) - 1 - axis_at))
    return gain


def bell_draw(stream_key, shape, scale, most, shards=(), kind=jnp.bfloat16):
    drawn = jax.random.normal(stream_key, shape, jnp.float32) * scale
    if len(shards) > 0:
        drawn = steps_of(stream_key, shape, shards, -0.22, 0.18) * drawn
    return jnp.clip(drawn, min=-most, max=most).astype(kind)


def setup_inputs(seed: int = 0) -> dict:
    splits = jax.random.split(jax.random.key(seed), 10)
    return {
        "thermal_anomaly": bell_draw(splits[0], (VERTICAL_LAYERS, MERIDIAN_CELLS, PARALLEL_CELLS), 1.0, 6.0, ((1, 4), (2, 8)), jnp.float32),
        "saltiness_anomaly": bell_draw(splits[1], (VERTICAL_LAYERS, MERIDIAN_CELLS, PARALLEL_CELLS), 1.0, 6.0, ((1, 4), (2, 8)), jnp.float32),
        "zonal_current": bell_draw(splits[2], (VERTICAL_LAYERS, MERIDIAN_CELLS, PARALLEL_CELLS), 0.3, 1.8, ((1, 4), (2, 8)), jnp.float32),
        "meridional_current": bell_draw(splits[3], (VERTICAL_LAYERS, MERIDIAN_CELLS, PARALLEL_CELLS), 0.3, 1.8, ((1, 4), (2, 8)), jnp.float32),
        "free_elevation": bell_draw(splits[4], (MERIDIAN_CELLS, PARALLEL_CELLS), 0.3, 1.8, ((0, 4), (1, 8)), jnp.float32),
        "zonal_traction": bell_draw(splits[5], (MERIDIAN_CELLS, PARALLEL_CELLS), 1.0, 6.0, ((0, 4), (1, 8)), jnp.float32),
        "meridional_traction": bell_draw(splits[6], (MERIDIAN_CELLS, PARALLEL_CELLS), 1.0, 6.0, ((0, 4), (1, 8)), jnp.float32),
        "water_indicator": set_ends((jax.random.randint(splits[7], (MERIDIAN_CELLS, PARALLEL_CELLS), 0, 5) < 4).astype(jnp.int32), jax.random.fold_in(splits[7], 1), 0, 1),
        "bottom_layer_index": set_ends(jax.random.randint(splits[8], (MERIDIAN_CELLS, PARALLEL_CELLS), 1, VERTICAL_LAYERS + 1), jax.random.fold_in(splits[8], 1), 1, VERTICAL_LAYERS).astype(jnp.int32),
    }


TIME_STEP = 0.4
TRACER_DIFF = 0.05
MOMENTUM_DIFF = 0.05
BOTTOM_DRAG = 0.05
WIND_FACTOR = 0.5
CORIOLIS_SCALE = 0.5
LATITUDE_SPAN = 2.6
GRAVITY_FACTOR = 0.3
THERMAL_COEF = 0.2
HALINE_COEF = 0.8
BACKGROUND_MIX = 0.05
CONVECTIVE_MIX = 1.5
STABILITY_FACTOR = 5.0
HEIGHT_FACTOR = 0.2
SLOPE_FACTOR = 0.15


def offset_view(field, margin, shift_lat, shift_lon, meridional_cell_count, zonal_cell_count):
    return field[..., margin + shift_lat:margin + shift_lat + meridional_cell_count, margin + shift_lon:margin + shift_lon + zonal_cell_count]


def column_solve(couplings, first, second, layered_profile):
    zero_plane = jnp.zeros_like(first[0])
    ratios = []
    parts_first = []
    parts_second = []
    for layer in range(layered_profile):
        lower = couplings[layer - 1] if layer > 0 else zero_plane
        upper = couplings[layer] if layer < layered_profile - 1 else zero_plane
        denom = 1.0 + lower + upper
        rhs_first = first[layer]
        rhs_second = second[layer]
        if layer > 0:
            denom = denom - lower * ratios[-1]
            rhs_first = rhs_first + lower * parts_first[-1]
            rhs_second = rhs_second + lower * parts_second[-1]
        ratios.append(upper / denom)
        parts_first.append(rhs_first / denom)
        parts_second.append(rhs_second / denom)
    out_first = list(parts_first)
    out_second = list(parts_second)
    for layer in reversed(range(layered_profile - 1)):
        out_first[layer] = parts_first[layer] + ratios[layer] * out_first[layer + 1]
        out_second[layer] = parts_second[layer] + ratios[layer] * out_second[layer + 1]
    return jnp.stack(out_first), jnp.stack(out_second)


def advance_stratified_flow(tem, sal, uvel, vvel, vertical_layer_count, tracer_pad, flow_pad, lat_first, meridional_cell_count, zonal_cell_count, zonal_traction, meridional_traction, lat_total):
    layered_profile = tem.shape[0]
    level_index = jnp.arange(layered_profile, dtype=jnp.float32)[:, None, None]

    def wet_at(shift_lat, shift_lon):
        return jnp.clip(offset_view(vertical_layer_count, tracer_pad, shift_lat, shift_lon, meridional_cell_count, zonal_cell_count)[None] - level_index, 0.0, 1.0)

    def tracer_at(field, shift_lat, shift_lon):
        return offset_view(field, tracer_pad, shift_lat, shift_lon, meridional_cell_count, zonal_cell_count) * wet_at(shift_lat, shift_lon)

    def east_flow(shift_lat, shift_lon):
        return offset_view(uvel, flow_pad, shift_lat, shift_lon, meridional_cell_count, zonal_cell_count) * wet_at(shift_lat, shift_lon) * wet_at(shift_lat, shift_lon + 1)

    def north_flow(shift_lat, shift_lon):
        return offset_view(vvel, flow_pad, shift_lat, shift_lon, meridional_cell_count, zonal_cell_count) * wet_at(shift_lat, shift_lon) * wet_at(shift_lat + 1, shift_lon)

    def east_flux(field, shift_lon):
        far_west = tracer_at(field, 0, shift_lon - 1)
        near_west = tracer_at(field, 0, shift_lon)
        near_east = tracer_at(field, 0, shift_lon + 1)
        far_east = tracer_at(field, 0, shift_lon + 2)
        speed = east_flow(0, shift_lon)
        centred = speed * (7.0 * (near_west + near_east) - (far_west + far_east)) / 12.0
        upwind = jnp.abs(speed) * (3.0 * (near_west - near_east) - (far_west - far_east)) / 12.0
        mixing = TRACER_DIFF * (near_east - near_west) * wet_at(0, shift_lon) * wet_at(0, shift_lon + 1)
        return centred - upwind - mixing

    def north_flux(field, shift_lat):
        far_south = tracer_at(field, shift_lat - 1, 0)
        near_south = tracer_at(field, shift_lat, 0)
        near_north = tracer_at(field, shift_lat + 1, 0)
        far_north = tracer_at(field, shift_lat + 2, 0)
        speed = north_flow(shift_lat, 0)
        centred = speed * (7.0 * (near_south + near_north) - (far_south + far_north)) / 12.0
        upwind = jnp.abs(speed) * (3.0 * (near_south - near_north) - (far_south - far_north)) / 12.0
        mixing = TRACER_DIFF * (near_north - near_south) * wet_at(shift_lat, 0) * wet_at(shift_lat + 1, 0)
        return centred - upwind - mixing

    def advect(field):
        return tracer_at(field, 0, 0) - TIME_STEP * (east_flux(field, 0) - east_flux(field, -1) + north_flux(field, 0) - north_flux(field, -1))

    tem_star = advect(tem)
    sal_star = advect(sal)
    wet_here = wet_at(0, 0)
    dens_star = HALINE_COEF * sal_star - THERMAL_COEF * tem_star
    couplings = []
    for layer in range(layered_profile - 1):
        rise = jnp.maximum(dens_star[layer + 1] - dens_star[layer], 0.0)
        couplings.append(TIME_STEP * (BACKGROUND_MIX + CONVECTIVE_MIX / (1.0 + STABILITY_FACTOR * rise)) * wet_here[layer + 1])
    tem_new, sal_new = column_solve(couplings, tem_star, sal_star, layered_profile)

    def pressure_at(shift_lat, shift_lon):
        dens = HALINE_COEF * tracer_at(sal, shift_lat, shift_lon) - THERMAL_COEF * tracer_at(tem, shift_lat, shift_lon)
        return GRAVITY_FACTOR * (jnp.cumsum(dens, axis=0) - 0.5 * dens)

    press = pressure_at(0, 0)
    grad_x = pressure_at(0, 1) - press
    grad_y = pressure_at(1, 0) - press
    rows_global = lat_first + jnp.arange(meridional_cell_count, dtype=jnp.float32)
    coriolis_u = (CORIOLIS_SCALE * jnp.sin(LATITUDE_SPAN * ((rows_global + 0.5) / lat_total - 0.5)))[:, None]
    coriolis_v = (CORIOLIS_SCALE * jnp.sin(LATITUDE_SPAN * ((rows_global + 1.0) / lat_total - 0.5)))[:, None]
    u_here = east_flow(0, 0)
    v_here = north_flow(0, 0)
    v_at_u = 0.25 * (north_flow(0, 0) + north_flow(0, 1) + north_flow(-1, 0) + north_flow(-1, 1))
    u_at_v = 0.25 * (east_flow(0, 0) + east_flow(0, -1) + east_flow(1, 0) + east_flow(1, -1))
    lap_u = east_flow(0, 1) + east_flow(0, -1) + east_flow(1, 0) + east_flow(-1, 0) - 4.0 * u_here
    lap_v = north_flow(0, 1) + north_flow(0, -1) + north_flow(1, 0) + north_flow(-1, 0) - 4.0 * v_here
    open_u = wet_here * wet_at(0, 1)
    open_v = wet_here * wet_at(1, 0)
    surface = (jnp.arange(layered_profile) == 0).astype(jnp.float32)[:, None, None]
    u_trial = open_u * (u_here + TIME_STEP * (coriolis_u * v_at_u - grad_x + MOMENTUM_DIFF * lap_u - BOTTOM_DRAG * u_here) + TIME_STEP * WIND_FACTOR * surface * zonal_traction)
    v_trial = open_v * (v_here + TIME_STEP * (-coriolis_v * u_at_v - grad_y + MOMENTUM_DIFF * lap_v - BOTTOM_DRAG * v_here) + TIME_STEP * WIND_FACTOR * surface * meridional_traction)
    return (tem_new, sal_new, u_trial, v_trial, open_u, open_v,
            jnp.sum(u_trial - u_here, axis=0), jnp.sum(v_trial - v_here, axis=0),
            jnp.sum(u_here, axis=0), jnp.sum(v_here, axis=0),
            jnp.sum(open_u, axis=0), jnp.sum(open_v, axis=0))


def finish(trial, opening, face_depth, transport):
    return opening * (trial + (transport - jnp.sum(trial, axis=0)) / jnp.maximum(face_depth, 1.0))


def extend_border_cells(field, width):
    beside_all = jnp.concatenate([field[..., -width:], field, field[..., :width]], axis=-1)
    pads = [(0, 0)] * (field.ndim - 2) + [(width, width), (0, 0)]
    return jnp.pad(beside_all, pads)


def neighbour(field, shift_lat, shift_lon):
    rolled = jnp.roll(field, -shift_lon, axis=-1)
    padded = jnp.pad(rolled, ((1, 1), (0, 0)))
    return padded[1 + shift_lat:1 + shift_lat + field.shape[0]]


def reference(thermal_anomaly, saltiness_anomaly, zonal_current, meridional_current, free_elevation, zonal_traction, meridional_traction, water_indicator, bottom_layer_index):
    vertical_layer_count = (water_indicator * bottom_layer_index).astype(jnp.float32)
    advanced_state = advance_stratified_flow(extend_border_cells(thermal_anomaly, 2), extend_border_cells(saltiness_anomaly, 2), extend_border_cells(zonal_current, 2), extend_border_cells(meridional_current, 2),
                         extend_border_cells(vertical_layer_count, 2), 2, 2, jnp.float32(0.0), MERIDIAN_CELLS, PARALLEL_CELLS, zonal_traction, meridional_traction, MERIDIAN_CELLS)
    tem_new, sal_new, u_trial, v_trial, open_u, open_v, force_u, force_v, big_u, big_v, depth_u, depth_v = advanced_state
    mouth_u = jnp.minimum(depth_u, 1.0)
    mouth_v = jnp.minimum(depth_v, 1.0)
    height = free_elevation
    for substep in range(NSUB):
        height = height - HEIGHT_FACTOR * (big_u - neighbour(big_u, 0, -1) + big_v - neighbour(big_v, -1, 0))
        big_u = mouth_u * (big_u + force_u / NSUB - SLOPE_FACTOR * depth_u * (neighbour(height, 0, 1) - height))
        big_v = mouth_v * (big_v + force_v / NSUB - SLOPE_FACTOR * depth_v * (neighbour(height, 1, 0) - height))
    u_next = finish(u_trial, open_u, depth_u, big_u)
    v_next = finish(v_trial, open_v, depth_v, big_v)
    return tem_new, sal_new, u_next, v_next, height, big_u, big_v
```

```python
import functools

import jax
import jax.numpy as jnp
from jax import lax
from jax.experimental import pallas as pl
from jax.experimental.pallas import tpu as pltpu
from jax.sharding import PartitionSpec as P

NSUB = 4
TIME_STEP = 0.4
TRACER_DIFF = 0.05
MOMENTUM_DIFF = 0.05
BOTTOM_DRAG = 0.05
WIND_FACTOR = 0.5
CORIOLIS_SCALE = 0.5
LATITUDE_SPAN = 2.6
GRAVITY_FACTOR = 0.3
THERMAL_COEF = 0.2
HALINE_COEF = 0.8
BACKGROUND_MIX = 0.05
CONVECTIVE_MIX = 1.5
STABILITY_FACTOR = 5.0
HEIGHT_FACTOR = 0.2
SLOPE_FACTOR = 0.15

LANES = 128
SUB = 8
HALO_FIELDS = (2, 2, 1, 1)
HALO_DEPTH = 2
FLAT_HALO = NSUB
FLAT_FIELDS = 6
MESH = pl.DeviceIdType.MESH


def lane_shift(x, s):
    n = x.shape[-1]
    return pltpu.roll(x, (-s) % n, x.ndim - 1)


def row_shift(x, s):
    n = x.shape[0]
    return pltpu.roll(x, (-s) % n, 0)


def open_at(depth, k):
    return jnp.clip(depth - k, 0.0, 1.0)


def pack_strips(pieces, rows):
    lane = lax.broadcasted_iota(jnp.int32, (rows, LANES), 1)
    west = jnp.zeros((rows, LANES), jnp.float32)
    east = jnp.zeros((rows, LANES), jnp.float32)
    for first, last, width, at in pieces:
        mask = (lane >= at) & (lane < at + width)
        west = jnp.where(mask, pltpu.roll(first, at, 1) if at else first, west)
        east = jnp.where(mask, pltpu.roll(last, (at + width) % LANES, 1), east)
    return west, east


def halo_tile(from_east, from_west, width, at):
    lane = lax.broadcasted_iota(jnp.int32, from_east.shape, 1)
    return jnp.where(
        lane < LANES // 2,
        pltpu.roll(from_east, (-at) % LANES, 1),
        pltpu.roll(from_west, (-at - width) % LANES, 1),
    )


def kernel(
    lat_total,
    t_in, s_in, u_in, v_in, eta_in, zt_in, mt_in, wi_in, bi_in,
    t_out, s_out, u_out, v_out, eta_out, tx_out, ty_out,
    te, se, ue, ve, de, hue, hve, flat, ratio, fu_ref, fv_ref,
    west1, east1, north1, south1, fe1, fw1, fn1, fs1,
    west2, east2, north2, south2, fe2, fw2, fn2, fs2,
    load_sem, send1, recv1, send2, recv2,
):
    levels, rows, cols = t_out.shape
    lon, lat = lax.axis_index("lon"), lax.axis_index("lat")
    nlon, nlat = lax.axis_size("lon"), lax.axis_size("lat")
    wst, est = lax.rem(lon + nlon - 1, nlon), lax.rem(lon + 1, nlon)
    nth, sth = lax.rem(lat + 1, nlat), lax.rem(lat + nlat - 1, nlat)
    has_n, has_s = lat < nlat - 1, lat > 0
    top, bot = rows, SUB
    end = SUB + rows

    loads = []
    for n, (src, dst) in enumerate(((t_in, te), (s_in, se), (u_in, ue), (v_in, ve))):
        loads.append(pltpu.make_async_copy(src, dst.at[:, SUB:end, 0:cols], load_sem.at[n]))
        loads[-1].start()

    barrier = pltpu.get_barrier_semaphore()

    def greet(lo, la):
        pl.semaphore_signal(barrier, inc=1, device_id=(lo, la), device_id_type=MESH)

    greet(wst, lat)
    greet(est, lat)

    @pl.when(has_n)
    def _():
        greet(wst, nth)
        greet(lon, nth)
        greet(est, nth)

    @pl.when(has_s)
    def _():
        greet(wst, sth)
        greet(lon, sth)
        greet(est, sth)

    def exchange(west, east, north, south, fe, fw, fn, fs, send, recv):
        def cp(n, src, dst, lo, la):
            return pltpu.make_async_remote_copy(
                src_ref=src, dst_ref=dst, send_sem=send.at[n], recv_sem=recv.at[n],
                device_id=(lo, la), device_id_type=MESH)

        lo_s, hi_s = pl.ds(0, SUB), pl.ds(rows - SUB, SUB)
        own, below, above = pl.ds(SUB, rows), pl.ds(0, SUB), pl.ds(end, SUB)
        along = [cp(0, west, fe.at[own], wst, lat), cp(1, east, fw.at[own], est, lat)]
        up = [cp(2, north, fs, lon, nth),
              cp(3, west.at[hi_s], fe.at[below], wst, nth),
              cp(4, east.at[hi_s], fw.at[below], est, nth)]
        down = [cp(5, south, fn, lon, sth),
                cp(6, west.at[lo_s], fe.at[above], wst, sth),
                cp(7, east.at[lo_s], fw.at[above], est, sth)]

        def start():
            @pl.when(has_n)
            def _():
                for c in up:
                    c.start()

            @pl.when(has_s)
            def _():
                for c in down:
                    c.start()

            for c in along:
                c.start()

        def finish():
            for c in along:
                c.wait_recv()
                c.wait_send()

            @pl.when(has_n)
            def _():
                for c in up:
                    c.wait_send()
                for c in down:
                    c.wait_recv()

            @pl.when(has_s)
            def _():
                for c in down:
                    c.wait_send()
                for c in up:
                    c.wait_recv()

        return start, finish

    def clear_edges(fe, fw, fn, fs):
        @pl.when(jnp.logical_not(has_n))
        def _():
            fn[...] = jnp.zeros_like(fn)
            fe[end:, :] = jnp.zeros((SUB, LANES), jnp.float32)
            fw[end:, :] = jnp.zeros((SUB, LANES), jnp.float32)

        @pl.when(jnp.logical_not(has_s))
        def _():
            fs[...] = jnp.zeros_like(fs)
            fe[:SUB, :] = jnp.zeros((SUB, LANES), jnp.float32)
            fw[:SUB, :] = jnp.zeros((SUB, LANES), jnp.float32)

    depth = (wi_in[...] * bi_in[...]).astype(jnp.float32)
    de[SUB:end, 0:cols] = depth
    clear_edges(fe1, fw1, fn1, fs1)
    clear_edges(fe2, fw2, fn2, fs2)
    row = lax.broadcasted_iota(jnp.int32, (rows, LANES), 0).astype(jnp.float32)
    row = row + (lat * rows).astype(jnp.float32)
    fu_ref[...] = CORIOLIS_SCALE * jnp.sin(LATITUDE_SPAN * ((row + 0.5) / lat_total - 0.5))
    fv_ref[...] = CORIOLIS_SCALE * jnp.sin(LATITUDE_SPAN * ((row + 1.0) / lat_total - 0.5))

    for c in loads:
        c.wait()

    fields = (te, se, ue, ve)
    per_level = sum(HALO_FIELDS)
    depth_at = per_level * levels
    places = []
    for k in range(levels):
        at = per_level * k
        for ref, width in zip(fields, HALO_FIELDS):
            places.append((ref, k, width, at))
            at += width
    for ref, k, width, at in places:
        south1[at:at + width, :] = ref[k, SUB:SUB + width, 0:cols]
        north1[at:at + width, :] = ref[k, end - width:end, 0:cols]
    south1[depth_at:depth_at + HALO_DEPTH, :] = depth[:HALO_DEPTH]
    north1[depth_at:depth_at + HALO_DEPTH, :] = depth[rows - HALO_DEPTH:]
    pieces = [(ref[k, SUB:end, 0:LANES], ref[k, SUB:end, cols - LANES:cols], width, at)
              for ref, k, width, at in places]
    pieces.append((depth[:, :LANES], depth[:, cols - LANES:], HALO_DEPTH, depth_at))
    west, east = pack_strips(pieces, rows)
    west1[...] = west
    east1[...] = east

    pl.semaphore_wait(barrier, 2 + 3 * has_n.astype(jnp.int32) + 3 * has_s.astype(jnp.int32))

    start1, finish1 = exchange(west1, east1, north1, south1, fe1, fw1, fn1, fs1, send1, recv1)
    start1()
    finish1()

    fe, fw = fe1[...], fw1[...]
    for ref, k, width, at in places:
        ref[k, :, cols:] = halo_tile(fe, fw, width, at)
        ref[k, SUB - width:SUB, 0:cols] = fs1[at:at + width, :]
        ref[k, end:end + width, 0:cols] = fn1[at:at + width, :]
    de[:, cols:] = halo_tile(fe, fw, HALO_DEPTH, depth_at)
    de[SUB - HALO_DEPTH:SUB, 0:cols] = fs1[depth_at:depth_at + HALO_DEPTH, :]
    de[end:end + HALO_DEPTH, 0:cols] = fn1[depth_at:depth_at + HALO_DEPTH, :]

    d = de[...]
    hue[...] = jnp.minimum(d, lane_shift(d, 1))
    hve[...] = jnp.minimum(d, row_shift(d, 1))

    @pl.loop(0, levels)
    def _(k):
        kf = k.astype(jnp.float32)
        wet = open_at(de[...], kf)
        te[k] = te[k] * wet
        se[k] = se[k] * wet
        ue[k] = ue[k] * open_at(hue[...], kf)
        ve[k] = ve[k] * open_at(hve[...], kf)

    for r in range(0, rows, SUB):
        here = slice(SUB + r, 2 * SUB + r)
        above = slice(SUB + r + 1, 2 * SUB + r + 1)
        below = slice(SUB + r - 1, 2 * SUB + r - 1)
        out = slice(r, r + SUB)
        fu = jnp.broadcast_to(fu_ref[out, 0:1], (SUB, cols))
        fv = jnp.broadcast_to(fv_ref[out, 0:1], (SUB, cols))

        def momentum(k, carry):
            cgx, cgy, su, sv, gu, gv = carry
            kf = k.astype(jnp.float32)
            wind = jnp.where(k == 0, TIME_STEP * WIND_FACTOR, 0.0)
            uw, un, us = ue[k, here, :], ue[k, above, :], ue[k, below, 0:cols]
            vw, vn, vs = ve[k, here, :], ve[k, above, 0:cols], ve[k, below, :]
            u, v = uw[:, :cols], vw[:, :cols]
            a = vw + vs
            b = uw + un
            v_at_u = 0.25 * (a[:, :cols] + lane_shift(a, 1)[:, :cols])
            u_at_v = 0.25 * (b[:, :cols] + lane_shift(b, -1)[:, :cols])
            lap_u = lane_shift(uw, 1)[:, :cols] + lane_shift(uw, -1)[:, :cols] + un[:, :cols] + us - 4.0 * u
            lap_v = lane_shift(vw, 1)[:, :cols] + lane_shift(vw, -1)[:, :cols] + vn + vs[:, :cols] - 4.0 * v
            rho = HALINE_COEF * se[k, here, :] - THERMAL_COEF * te[k, here, :]
            rho_n = HALINE_COEF * se[k, above, 0:cols] - THERMAL_COEF * te[k, above, 0:cols]
            gx = lane_shift(rho, 1)[:, :cols] - rho[:, :cols]
            gy = rho_n - rho[:, :cols]
            cgx = cgx + gx
            cgy = cgy + gy
            px = GRAVITY_FACTOR * (cgx - 0.5 * gx)
            py = GRAVITY_FACTOR * (cgy - 0.5 * gy)
            mu = open_at(hue[here, 0:cols], kf)
            mv = open_at(hve[here, 0:cols], kf)
            ut = mu * (u + TIME_STEP * (fu * v_at_u - px + MOMENTUM_DIFF * lap_u - BOTTOM_DRAG * u)
                       + wind * zt_in[out, :])
            vt = mv * (v + TIME_STEP * (-fv * u_at_v - py + MOMENTUM_DIFF * lap_v - BOTTOM_DRAG * v)
                       + wind * mt_in[out, :])
            u_out[k, out, :] = ut
            v_out[k, out, :] = vt
            return cgx, cgy, su + u, sv + v, gu + (ut - u), gv + (vt - v)

        zero = jnp.zeros((SUB, cols), jnp.float32)
        _, _, su, sv, gu, gv = lax.fori_loop(0, levels, momentum, (zero,) * 6)
        flat[0, here, 0:cols] = eta_in[out, :]
        flat[1, here, 0:cols] = su
        flat[2, here, 0:cols] = sv
        flat[3, here, 0:cols] = gu
        flat[4, here, 0:cols] = gv
        flat[5, here, 0:cols] = de[here, 0:cols]

    pieces = []
    for f in range(FLAT_FIELDS):
        at = FLAT_HALO * f
        south2[at:at + FLAT_HALO, :] = flat[f, SUB:SUB + FLAT_HALO, 0:cols]
        north2[at:at + FLAT_HALO, :] = flat[f, end - FLAT_HALO:end, 0:cols]
        pieces.append((flat[f, SUB:end, 0:LANES], flat[f, SUB:end, cols - LANES:cols], FLAT_HALO, at))
    west, east = pack_strips(pieces, rows)
    west2[...] = west
    east2[...] = east
    start2, finish2 = exchange(west2, east2, north2, south2, fe2, fw2, fn2, fs2, send2, recv2)
    start2()

    for r in range(0, rows, SUB):
        here = slice(SUB + r, 2 * SUB + r)
        out = slice(r, r + SUB)

        def at_rows(s):
            return slice(SUB + r + s, 2 * SUB + r + s)

        def star(k):
            kf = k.astype(jnp.float32) if hasattr(k, "astype") else jnp.float32(k)
            uw = ue[k, here, :]
            v0 = ve[k, here, 0:cols]
            v1 = ve[k, at_rows(-1), 0:cols]
            up, un = jnp.maximum(uw, 0.0) * (1.0 / 6.0), jnp.minimum(uw, 0.0) * (1.0 / 6.0)
            v0p, v0n = jnp.maximum(v0, 0.0) * (1.0 / 6.0), jnp.minimum(v0, 0.0) * (1.0 / 6.0)
            v1p, v1n = jnp.maximum(v1, 0.0) * (1.0 / 6.0), jnp.minimum(v1, 0.0) * (1.0 / 6.0)
            mu = TRACER_DIFF * open_at(hue[here, :], kf)
            m0 = TRACER_DIFF * open_at(hve[here, 0:cols], kf)
            m1 = TRACER_DIFF * open_at(hve[at_rows(-1), 0:cols], kf)
            res = []
            for ref in (te, se):
                c = ref[k, here, :]
                cw, ce, cee = lane_shift(c, -1), lane_shift(c, 1), lane_shift(c, 2)
                fx = up * (2.0 * c + 5.0 * ce - cee) + un * (5.0 * c + 2.0 * ce - cw) - mu * (ce - c)
                dx = fx[:, :cols] - lane_shift(fx, -1)[:, :cols]
                c0 = c[:, :cols]
                ss, s1 = ref[k, at_rows(-2), 0:cols], ref[k, at_rows(-1), 0:cols]
                n1, nn = ref[k, at_rows(1), 0:cols], ref[k, at_rows(2), 0:cols]
                f0 = v0p * (2.0 * c0 + 5.0 * n1 - nn) + v0n * (5.0 * c0 + 2.0 * n1 - s1) - m0 * (n1 - c0)
                f1 = v1p * (2.0 * s1 + 5.0 * c0 - n1) + v1n * (5.0 * s1 + 2.0 * c0 - ss) - m1 * (c0 - s1)
                res.append(c0 - TIME_STEP * (dx + f0 - f1))
            return res

        def eliminate(k, t, s, lower, upper, rat, pt, ps):
            inv = 1.0 / (1.0 + upper + lower * (1.0 - rat))
            pt = (t + lower * pt) * inv
            ps = (s + lower * ps) * inv
            rat = upper * inv
            t_out[k, out, :] = pt
            s_out[k, out, :] = ps
            ratio[k, out, :] = rat
            return rat, pt, ps

        def forward(k, carry):
            t, s, lower, rat, pt, ps = carry
            tn, sn = star(k)
            rise = jnp.maximum(HALINE_COEF * (sn - s) - THERMAL_COEF * (tn - t), 0.0)
            mix = BACKGROUND_MIX + CONVECTIVE_MIX / (1.0 + STABILITY_FACTOR * rise)
            upper = TIME_STEP * mix * open_at(de[here, 0:cols], k.astype(jnp.float32))
            rat, pt, ps = eliminate(k - 1, t, s, lower, upper, rat, pt, ps)
            return tn, sn, upper, rat, pt, ps

        zero = jnp.zeros((SUB, cols), jnp.float32)
        t, s = star(0)
        t, s, lower, rat, pt, ps = lax.fori_loop(1, levels, forward, (t, s, zero, zero, zero, zero))
        rat, pt, ps = eliminate(levels - 1, t, s, lower, zero, rat, pt, ps)

        def backward(i, carry):
            t, s = carry
            k = levels - 2 - i
            rat = ratio[k, out, :]
            t = t_out[k, out, :] + rat * t
            s = s_out[k, out, :] + rat * s
            t_out[k, out, :] = t
            s_out[k, out, :] = s
            return t, s

        lax.fori_loop(0, levels - 1, backward, (pt, ps))

    finish2()

    fe, fw = fe2[...], fw2[...]
    for f in range(FLAT_FIELDS):
        at = FLAT_HALO * f
        flat[f, :, cols:] = halo_tile(fe, fw, FLAT_HALO, at)
        flat[f, SUB - FLAT_HALO:SUB, 0:cols] = fs2[at:at + FLAT_HALO, :]
        flat[f, end:end + FLAT_HALO, 0:cols] = fn2[at:at + FLAT_HALO, :]
    eta, bu, bv = flat[0], flat[1], flat[2]
    su, sv = bu[SUB:end, :cols], bv[SUB:end, :cols]
    gu, gv, d = flat[3], flat[4], flat[5]
    hu = jnp.minimum(d, lane_shift(d, 1))
    hv = jnp.minimum(d, row_shift(d, 1))
    mouth_u, mouth_v = jnp.minimum(hu, 1.0), jnp.minimum(hv, 1.0)
    for _ in range(NSUB):
        eta = eta - HEIGHT_FACTOR * (bu - lane_shift(bu, -1) + bv - row_shift(bv, -1))
        bu = mouth_u * (bu + gu / NSUB - SLOPE_FACTOR * hu * (lane_shift(eta, 1) - eta))
        bv = mouth_v * (bv + gv / NSUB - SLOPE_FACTOR * hv * (row_shift(eta, 1) - eta))
    eta_out[...] = eta[SUB:end, :cols]
    tu, tv = bu[SUB:end, :cols], bv[SUB:end, :cols]
    tx_out[...] = tu
    ty_out[...] = tv
    hu, hv = hu[SUB:end, :cols], hv[SUB:end, :cols]
    flat[0, SUB:end, :cols] = (tu - (gu[SUB:end, :cols] + su)) / jnp.maximum(hu, 1.0)
    flat[1, SUB:end, :cols] = (tv - (gv[SUB:end, :cols] + sv)) / jnp.maximum(hv, 1.0)

    @pl.loop(0, levels)
    def _(k):
        kf = k.astype(jnp.float32)
        u_out[k] = open_at(hue[SUB:end, :cols], kf) * (u_out[k] + flat[0, SUB:end, :cols])
        v_out[k] = open_at(hve[SUB:end, :cols], kf) * (v_out[k] + flat[1, SUB:end, :cols])


def body(*args):
    levels, rows, cols = args[0].shape
    f32 = jnp.float32
    cube = jax.ShapeDtypeStruct((levels, rows, cols), f32)
    plane = jax.ShapeDtypeStruct((rows, cols), f32)
    erows, ecols = rows + 2 * SUB, cols + LANES
    send_rows = -(-(sum(HALO_FIELDS) * levels + HALO_DEPTH) // SUB) * SUB
    flat_rows = FLAT_FIELDS * FLAT_HALO

    def buffers(n):
        strip, ext = pltpu.VMEM((rows, LANES), f32), pltpu.VMEM((erows, LANES), f32)
        block = pltpu.VMEM((n, cols), f32)
        return [strip, strip, block, block, ext, ext, block, block]

    vmem = pl.BlockSpec(memory_space=pltpu.VMEM)
    hbm = pl.BlockSpec(memory_space=pl.ANY)
    return pl.pallas_call(
        functools.partial(kernel, rows * lax.axis_size("lat")),
        out_shape=(cube,) * 4 + (plane,) * 3,
        in_specs=[hbm] * 4 + [vmem] * 5,
        out_specs=(vmem,) * 7,
        scratch_shapes=(
            [pltpu.VMEM((levels, erows, ecols), f32)] * 4
            + [pltpu.VMEM((erows, ecols), f32)] * 3
            + [pltpu.VMEM((FLAT_FIELDS, erows, ecols), f32),
               pltpu.VMEM((levels, rows, cols), f32)]
            + [pltpu.VMEM((rows, LANES), f32)] * 2
            + buffers(send_rows) + buffers(flat_rows)
            + [pltpu.SemaphoreType.DMA((4,))]
            + [pltpu.SemaphoreType.DMA((8,))] * 4
        ),
        compiler_params=pltpu.CompilerParams(
            collective_id=0, has_side_effects=True, vmem_limit_bytes=40 * 1024 * 1024),
    )(*args)


def solution(mesh):
    cube, plane = P(None, "lat", "lon"), P("lat", "lon")
    return jax.shard_map(
        body,
        mesh=mesh,
        in_specs=(cube,) * 4 + (plane,) * 5,
        out_specs=(cube,) * 4 + (plane,) * 3,
        check_vma=False,
    )
```

```python
import functools

import jax
import jax.numpy as jnp
from jax import lax
from jax.experimental import pallas as pl
from jax.experimental.pallas import tpu as pltpu
from jax.sharding import PartitionSpec as P

NSUB = 4
TIME_STEP = 0.4
TRACER_DIFF = 0.05
MOMENTUM_DIFF = 0.05
BOTTOM_DRAG = 0.05
WIND_FACTOR = 0.5
CORIOLIS_SCALE = 0.5
LATITUDE_SPAN = 2.6
GRAVITY_FACTOR = 0.3
THERMAL_COEF = 0.2
HALINE_COEF = 0.8
BACKGROUND_MIX = 0.05
CONVECTIVE_MIX = 1.5
STABILITY_FACTOR = 5.0
HEIGHT_FACTOR = 0.2
SLOPE_FACTOR = 0.15

LANES = 128
VMEM_BYTES = 67043328
SUB = 8
HALO_FIELDS = (2, 2, 1, 1)
HALO_DEPTH = 2
FLAT_HALO = NSUB
FLAT_FIELDS = 6
MESH = pl.DeviceIdType.MESH


def lane_shift(x, s):
    n = x.shape[-1]
    return pltpu.roll(x, (-s) % n, x.ndim - 1)


def row_shift(x, s):
    n = x.shape[0]
    return pltpu.roll(x, (-s) % n, 0)


def open_at(depth, k):
    return jnp.clip(depth - k, 0.0, 1.0)


def pack_strips(pieces, rows):
    lane = lax.broadcasted_iota(jnp.int32, (rows, LANES), 1)
    west = jnp.zeros((rows, LANES), jnp.float32)
    east = jnp.zeros((rows, LANES), jnp.float32)
    for first, last, width, at in pieces:
        mask = (lane >= at) & (lane < at + width)
        west = jnp.where(mask, pltpu.roll(first, at, 1) if at else first, west)
        east = jnp.where(mask, pltpu.roll(last, (at + width) % LANES, 1), east)
    return west, east


def halo_tile(from_east, from_west, width, at):
    lane = lax.broadcasted_iota(jnp.int32, from_east.shape, 1)
    return jnp.where(
        lane < LANES // 2,
        pltpu.roll(from_east, (-at) % LANES, 1),
        pltpu.roll(from_west, (-at - width) % LANES, 1),
    )


def kernel(
    lat_total,
    t_in, s_in, u_in, v_in, eta_hbm, zt_hbm, mt_hbm, wi_hbm, bi_hbm,
    t_hbm, s_hbm, u_hbm, v_hbm, flat_hbm,
    t_out, s_out, u_out, v_out, flat,
    te, se, ue, ve, de, hue, hve, ratio, fu_ref, fv_ref,
    eta_in, zt_in, mt_in, wi_in, bi_in,
    west1, east1, north1, south1, fe1, fw1, fn1, fs1,
    west2, east2, north2, south2, fe2, fw2, fn2, fs2,
    load_sem, store_sem, send1, recv1, send2, recv2,
):
    levels, rows, cols = t_out.shape
    lon, lat = lax.axis_index("lon"), lax.axis_index("lat")
    nlon, nlat = lax.axis_size("lon"), lax.axis_size("lat")
    wst, est = lax.rem(lon + nlon - 1, nlon), lax.rem(lon + 1, nlon)
    nth, sth = lax.rem(lat + 1, nlat), lax.rem(lat + nlat - 1, nlat)
    has_n, has_s = lat < nlat - 1, lat > 0
    top, bot = rows, SUB
    end = SUB + rows

    loads, stores = [], []

    def store_rows(n, src, dst, r):
        part = pl.ds(r, SUB)
        stores.append(pltpu.make_async_copy(src.at[:, part, :], dst.at[:, part, :], store_sem.at[n, r // SUB]))
        stores[-1].start()

    planes = ((wi_hbm, wi_in), (bi_hbm, bi_in), (eta_hbm, eta_in), (zt_hbm, zt_in), (mt_hbm, mt_in))
    cubes = ((t_in, te), (s_in, se), (u_in, ue), (v_in, ve))
    for n, (src, dst) in enumerate(planes):
        loads.append(pltpu.make_async_copy(src, dst, load_sem.at[n]))
    for n, (src, dst) in enumerate(cubes):
        loads.append(pltpu.make_async_copy(src, dst.at[:, SUB:end, 0:cols], load_sem.at[len(planes) + n]))
    for c in loads:
        c.start()

    barrier = pltpu.get_barrier_semaphore()

    def greet(lo, la):
        pl.semaphore_signal(barrier, inc=1, device_id=(lo, la), device_id_type=MESH)

    greet(wst, lat)
    greet(est, lat)

    @pl.when(has_n)
    def _():
        greet(wst, nth)
        greet(lon, nth)
        greet(est, nth)

    @pl.when(has_s)
    def _():
        greet(wst, sth)
        greet(lon, sth)
        greet(est, sth)

    def exchange(west, east, north, south, fe, fw, fn, fs, send, recv):
        def cp(n, src, dst, lo, la):
            return pltpu.make_async_remote_copy(
                src_ref=src, dst_ref=dst, send_sem=send.at[n], recv_sem=recv.at[n],
                device_id=(lo, la), device_id_type=MESH)

        lo_s, hi_s = pl.ds(0, SUB), pl.ds(rows - SUB, SUB)
        own, below, above = pl.ds(SUB, rows), pl.ds(0, SUB), pl.ds(end, SUB)
        along = [cp(0, west, fe.at[own], wst, lat), cp(1, east, fw.at[own], est, lat)]
        up = [cp(2, north, fs, lon, nth),
              cp(3, west.at[hi_s], fe.at[below], wst, nth),
              cp(4, east.at[hi_s], fw.at[below], est, nth)]
        down = [cp(5, south, fn, lon, sth),
                cp(6, west.at[lo_s], fe.at[above], wst, sth),
                cp(7, east.at[lo_s], fw.at[above], est, sth)]

        def start():
            @pl.when(has_n)
            def _():
                for c in up:
                    c.start()

            @pl.when(has_s)
            def _():
                for c in down:
                    c.start()

            for c in along:
                c.start()

        def finish():
            for c in along:
                c.wait_recv()
                c.wait_send()

            @pl.when(has_n)
            def _():
                for c in up:
                    c.wait_send()
                for c in down:
                    c.wait_recv()

            @pl.when(has_s)
            def _():
                for c in down:
                    c.wait_send()
                for c in up:
                    c.wait_recv()

        return start, finish

    def clear_edges(fe, fw, fn, fs):
        @pl.when(jnp.logical_not(has_n))
        def _():
            fn[...] = jnp.zeros_like(fn)
            fe[end:, :] = jnp.zeros((SUB, LANES), jnp.float32)
            fw[end:, :] = jnp.zeros((SUB, LANES), jnp.float32)

        @pl.when(jnp.logical_not(has_s))
        def _():
            fs[...] = jnp.zeros_like(fs)
            fe[:SUB, :] = jnp.zeros((SUB, LANES), jnp.float32)
            fw[:SUB, :] = jnp.zeros((SUB, LANES), jnp.float32)

    clear_edges(fe1, fw1, fn1, fs1)
    clear_edges(fe2, fw2, fn2, fs2)
    row = lax.broadcasted_iota(jnp.int32, (rows, LANES), 0).astype(jnp.float32)
    row = row + (lat * rows).astype(jnp.float32)
    fu_ref[...] = CORIOLIS_SCALE * jnp.sin(LATITUDE_SPAN * ((row + 0.5) / lat_total - 0.5))
    fv_ref[...] = CORIOLIS_SCALE * jnp.sin(LATITUDE_SPAN * ((row + 1.0) / lat_total - 0.5))

    for c in loads:
        c.wait()
    depth = (wi_in[...] * bi_in[...]).astype(jnp.float32)
    de[SUB:end, 0:cols] = depth

    fields = (te, se, ue, ve)
    per_level = sum(HALO_FIELDS)
    depth_at = per_level * levels
    places = []
    for k in range(levels):
        at = per_level * k
        for ref, width in zip(fields, HALO_FIELDS):
            places.append((ref, k, width, at))
            at += width
    for ref, k, width, at in places:
        south1[at:at + width, :] = ref[k, SUB:SUB + width, 0:cols]
        north1[at:at + width, :] = ref[k, end - width:end, 0:cols]
    south1[depth_at:depth_at + HALO_DEPTH, :] = depth[:HALO_DEPTH]
    north1[depth_at:depth_at + HALO_DEPTH, :] = depth[rows - HALO_DEPTH:]
    pieces = [(ref[k, SUB:end, 0:LANES], ref[k, SUB:end, cols - LANES:cols], width, at)
              for ref, k, width, at in places]
    pieces.append((depth[:, :LANES], depth[:, cols - LANES:], HALO_DEPTH, depth_at))
    west, east = pack_strips(pieces, rows)
    west1[...] = west
    east1[...] = east

    pl.semaphore_wait(barrier, 2 + 3 * has_n.astype(jnp.int32) + 3 * has_s.astype(jnp.int32))

    start1, finish1 = exchange(west1, east1, north1, south1, fe1, fw1, fn1, fs1, send1, recv1)
    start1()
    finish1()

    fe, fw = fe1[...], fw1[...]
    for ref, k, width, at in places:
        ref[k, :, cols:] = halo_tile(fe, fw, width, at)
        ref[k, SUB - width:SUB, 0:cols] = fs1[at:at + width, :]
        ref[k, end:end + width, 0:cols] = fn1[at:at + width, :]
    de[:, cols:] = halo_tile(fe, fw, HALO_DEPTH, depth_at)
    de[SUB - HALO_DEPTH:SUB, 0:cols] = fs1[depth_at:depth_at + HALO_DEPTH, :]
    de[end:end + HALO_DEPTH, 0:cols] = fn1[depth_at:depth_at + HALO_DEPTH, :]

    d = de[...]
    hue[...] = jnp.minimum(d, lane_shift(d, 1))
    hve[...] = jnp.minimum(d, row_shift(d, 1))

    @pl.loop(0, levels)
    def _(k):
        kf = k.astype(jnp.float32)
        wet = open_at(de[...], kf)
        te[k] = te[k] * wet
        se[k] = se[k] * wet
        ue[k] = ue[k] * open_at(hue[...], kf)
        ve[k] = ve[k] * open_at(hve[...], kf)

    for r in range(0, rows, SUB):
        here = slice(SUB + r, 2 * SUB + r)
        above = slice(SUB + r + 1, 2 * SUB + r + 1)
        below = slice(SUB + r - 1, 2 * SUB + r - 1)
        out = slice(r, r + SUB)
        fu = jnp.broadcast_to(fu_ref[out, 0:1], (SUB, cols))
        fv = jnp.broadcast_to(fv_ref[out, 0:1], (SUB, cols))

        def momentum(k, carry):
            cgx, cgy, su, sv, gu, gv = carry
            kf = k.astype(jnp.float32)
            wind = jnp.where(k == 0, TIME_STEP * WIND_FACTOR, 0.0)
            uw, un, us = ue[k, here, :], ue[k, above, :], ue[k, below, 0:cols]
            vw, vn, vs = ve[k, here, :], ve[k, above, 0:cols], ve[k, below, :]
            u, v = uw[:, :cols], vw[:, :cols]
            a = vw + vs
            b = uw + un
            v_at_u = 0.25 * (a[:, :cols] + lane_shift(a, 1)[:, :cols])
            u_at_v = 0.25 * (b[:, :cols] + lane_shift(b, -1)[:, :cols])
            lap_u = lane_shift(uw, 1)[:, :cols] + lane_shift(uw, -1)[:, :cols] + un[:, :cols] + us - 4.0 * u
            lap_v = lane_shift(vw, 1)[:, :cols] + lane_shift(vw, -1)[:, :cols] + vn + vs[:, :cols] - 4.0 * v
            rho = HALINE_COEF * se[k, here, :] - THERMAL_COEF * te[k, here, :]
            rho_n = HALINE_COEF * se[k, above, 0:cols] - THERMAL_COEF * te[k, above, 0:cols]
            gx = lane_shift(rho, 1)[:, :cols] - rho[:, :cols]
            gy = rho_n - rho[:, :cols]
            cgx = cgx + gx
            cgy = cgy + gy
            px = GRAVITY_FACTOR * (cgx - 0.5 * gx)
            py = GRAVITY_FACTOR * (cgy - 0.5 * gy)
            mu = open_at(hue[here, 0:cols], kf)
            mv = open_at(hve[here, 0:cols], kf)
            ut = mu * (u + TIME_STEP * (fu * v_at_u - px + MOMENTUM_DIFF * lap_u - BOTTOM_DRAG * u)
                       + wind * zt_in[out, :])
            vt = mv * (v + TIME_STEP * (-fv * u_at_v - py + MOMENTUM_DIFF * lap_v - BOTTOM_DRAG * v)
                       + wind * mt_in[out, :])
            u_out[k, out, :] = ut
            v_out[k, out, :] = vt
            return cgx, cgy, su + u, sv + v, gu + (ut - u), gv + (vt - v)

        zero = jnp.zeros((SUB, cols), jnp.float32)
        _, _, su, sv, gu, gv = lax.fori_loop(0, levels, momentum, (zero,) * 6)
        store_rows(0, u_out, u_hbm, r)
        store_rows(1, v_out, v_hbm, r)
        flat[0, here, 0:cols] = eta_in[out, :]
        flat[1, here, 0:cols] = su
        flat[2, here, 0:cols] = sv
        flat[3, here, 0:cols] = gu
        flat[4, here, 0:cols] = gv
        flat[5, here, 0:cols] = de[here, 0:cols]

    pieces = []
    for f in range(FLAT_FIELDS):
        at = FLAT_HALO * f
        south2[at:at + FLAT_HALO, :] = flat[f, SUB:SUB + FLAT_HALO, 0:cols]
        north2[at:at + FLAT_HALO, :] = flat[f, end - FLAT_HALO:end, 0:cols]
        pieces.append((flat[f, SUB:end, 0:LANES], flat[f, SUB:end, cols - LANES:cols], FLAT_HALO, at))
    west, east = pack_strips(pieces, rows)
    west2[...] = west
    east2[...] = east
    start2, finish2 = exchange(west2, east2, north2, south2, fe2, fw2, fn2, fs2, send2, recv2)
    start2()

    for r in range(0, rows, SUB):
        here = slice(SUB + r, 2 * SUB + r)
        out = slice(r, r + SUB)

        def at_rows(s):
            return slice(SUB + r + s, 2 * SUB + r + s)

        def star(k):
            kf = k.astype(jnp.float32) if hasattr(k, "astype") else jnp.float32(k)
            uw = ue[k, here, :]
            v0 = ve[k, here, 0:cols]
            v1 = ve[k, at_rows(-1), 0:cols]
            up, un = jnp.maximum(uw, 0.0) * (1.0 / 6.0), jnp.minimum(uw, 0.0) * (1.0 / 6.0)
            v0p, v0n = jnp.maximum(v0, 0.0) * (1.0 / 6.0), jnp.minimum(v0, 0.0) * (1.0 / 6.0)
            v1p, v1n = jnp.maximum(v1, 0.0) * (1.0 / 6.0), jnp.minimum(v1, 0.0) * (1.0 / 6.0)
            mu = TRACER_DIFF * open_at(hue[here, :], kf)
            m0 = TRACER_DIFF * open_at(hve[here, 0:cols], kf)
            m1 = TRACER_DIFF * open_at(hve[at_rows(-1), 0:cols], kf)
            res = []
            for ref in (te, se):
                c = ref[k, here, :]
                cw, ce, cee = lane_shift(c, -1), lane_shift(c, 1), lane_shift(c, 2)
                fx = up * (2.0 * c + 5.0 * ce - cee) + un * (5.0 * c + 2.0 * ce - cw) - mu * (ce - c)
                dx = fx[:, :cols] - lane_shift(fx, -1)[:, :cols]
                c0 = c[:, :cols]
                ss, s1 = ref[k, at_rows(-2), 0:cols], ref[k, at_rows(-1), 0:cols]
                n1, nn = ref[k, at_rows(1), 0:cols], ref[k, at_rows(2), 0:cols]
                f0 = v0p * (2.0 * c0 + 5.0 * n1 - nn) + v0n * (5.0 * c0 + 2.0 * n1 - s1) - m0 * (n1 - c0)
                f1 = v1p * (2.0 * s1 + 5.0 * c0 - n1) + v1n * (5.0 * s1 + 2.0 * c0 - ss) - m1 * (c0 - s1)
                res.append(c0 - TIME_STEP * (dx + f0 - f1))
            return res

        def eliminate(k, t, s, lower, upper, rat, pt, ps):
            inv = 1.0 / (1.0 + upper + lower * (1.0 - rat))
            pt = (t + lower * pt) * inv
            ps = (s + lower * ps) * inv
            rat = upper * inv
            t_out[k, out, :] = pt
            s_out[k, out, :] = ps
            ratio[k, out, :] = rat
            return rat, pt, ps

        def forward(k, carry):
            t, s, lower, rat, pt, ps = carry
            tn, sn = star(k)
            rise = jnp.maximum(HALINE_COEF * (sn - s) - THERMAL_COEF * (tn - t), 0.0)
            mix = BACKGROUND_MIX + CONVECTIVE_MIX / (1.0 + STABILITY_FACTOR * rise)
            upper = TIME_STEP * mix * open_at(de[here, 0:cols], k.astype(jnp.float32))
            rat, pt, ps = eliminate(k - 1, t, s, lower, upper, rat, pt, ps)
            return tn, sn, upper, rat, pt, ps

        zero = jnp.zeros((SUB, cols), jnp.float32)
        t, s = star(0)
        t, s, lower, rat, pt, ps = lax.fori_loop(1, levels, forward, (t, s, zero, zero, zero, zero))
        rat, pt, ps = eliminate(levels - 1, t, s, lower, zero, rat, pt, ps)

        def backward(i, carry):
            t, s = carry
            k = levels - 2 - i
            rat = ratio[k, out, :]
            t = t_out[k, out, :] + rat * t
            s = s_out[k, out, :] + rat * s
            t_out[k, out, :] = t
            s_out[k, out, :] = s
            return t, s

        lax.fori_loop(0, levels - 1, backward, (pt, ps))
        store_rows(2, t_out, t_hbm, r)
        store_rows(3, s_out, s_hbm, r)

    finish2()

    fe, fw = fe2[...], fw2[...]
    for f in range(FLAT_FIELDS):
        at = FLAT_HALO * f
        flat[f, :, cols:] = halo_tile(fe, fw, FLAT_HALO, at)
        flat[f, SUB - FLAT_HALO:SUB, 0:cols] = fs2[at:at + FLAT_HALO, :]
        flat[f, end:end + FLAT_HALO, 0:cols] = fn2[at:at + FLAT_HALO, :]
    stores.append(pltpu.make_async_copy(flat, flat_hbm, load_sem.at[0]))
    stores[-1].start()
    for c in stores:
        c.wait()


def closing(
    t_old, s_old, u_old, v_old, flat_old,
    t_hbm, s_hbm, u_hbm, v_hbm, eta_hbm, tx_hbm, ty_hbm,
    t_in, s_in, u_in, v_in, flat,
    u_next, v_next, eta_out, tx_out, ty_out, corr, load_sem, sem, level_sem,
):
    levels, rows, cols = t_in.shape
    end = SUB + rows
    loads = []
    for n, (src, dst) in enumerate(
        ((flat_old, flat), (t_old, t_in), (s_old, s_in), (u_old, u_in), (v_old, v_in))
    ):
        loads.append(pltpu.make_async_copy(src, dst, load_sem.at[n]))
        loads[-1].start()
    stores = []
    loads[0].wait()

    eta, bu, bv = flat[0], flat[1], flat[2]
    su, sv = bu[SUB:end, :cols], bv[SUB:end, :cols]
    gu, gv, d = flat[3], flat[4], flat[5]
    hu = jnp.minimum(d, lane_shift(d, 1))
    hv = jnp.minimum(d, row_shift(d, 1))
    mouth_u, mouth_v = jnp.minimum(hu, 1.0), jnp.minimum(hv, 1.0)
    for _ in range(NSUB):
        eta = eta - HEIGHT_FACTOR * (bu - lane_shift(bu, -1) + bv - row_shift(bv, -1))
        bu = mouth_u * (bu + gu / NSUB - SLOPE_FACTOR * hu * (lane_shift(eta, 1) - eta))
        bv = mouth_v * (bv + gv / NSUB - SLOPE_FACTOR * hv * (row_shift(eta, 1) - eta))
    loads[1].wait()
    loads[2].wait()
    for n, (src, dst) in enumerate(((t_in, t_hbm), (s_in, s_hbm))):
        stores.append(pltpu.make_async_copy(src, dst, sem.at[n]))
        stores[-1].start()
    eta_out[...] = eta[SUB:end, :cols]
    tu, tv = bu[SUB:end, :cols], bv[SUB:end, :cols]
    tx_out[...] = tu
    ty_out[...] = tv
    for n, (src, dst) in enumerate(((eta_out, eta_hbm), (tx_out, tx_hbm), (ty_out, ty_hbm))):
        stores.append(pltpu.make_async_copy(src, dst, sem.at[2 + n]))
        stores[-1].start()
    hu, hv = hu[SUB:end, :cols], hv[SUB:end, :cols]
    corr[0] = (tu - (gu[SUB:end, :cols] + su)) / jnp.maximum(hu, 1.0)
    corr[1] = (tv - (gv[SUB:end, :cols] + sv)) / jnp.maximum(hv, 1.0)
    corr[2] = hu
    corr[3] = hv
    loads[3].wait()
    loads[4].wait()

    for k in range(levels):
        u_next[k] = open_at(corr[2], float(k)) * (u_in[k] + corr[0])
        v_next[k] = open_at(corr[3], float(k)) * (v_in[k] + corr[1])
        if k % 4 == 3 or k == levels - 1:
            part = pl.ds(k - k % 4, k % 4 + 1)
            for n, (src, dst) in enumerate(((u_next, u_hbm), (v_next, v_hbm))):
                stores.append(pltpu.make_async_copy(src.at[part], dst.at[part], level_sem.at[n, k // 4]))
                stores[-1].start()
    for c in stores:
        c.wait()


def body(*args):
    levels, rows, cols = args[0].shape
    f32 = jnp.float32
    cube = jax.ShapeDtypeStruct((levels, rows, cols), f32)
    plane = jax.ShapeDtypeStruct((rows, cols), f32)
    erows, ecols = rows + 2 * SUB, cols + LANES
    send_rows = -(-(sum(HALO_FIELDS) * levels + HALO_DEPTH) // SUB) * SUB
    flat_rows = FLAT_FIELDS * FLAT_HALO

    def buffers(n):
        strip, ext = pltpu.VMEM((rows, LANES), f32), pltpu.VMEM((erows, LANES), f32)
        block = pltpu.VMEM((n, cols), f32)
        return [strip, strip, block, block, ext, ext, block, block]

    vflat = pltpu.VMEM((FLAT_FIELDS, erows, ecols), f32)
    hbm = pl.BlockSpec(memory_space=pltpu.HBM)
    vplane, vcube = pltpu.VMEM((rows, cols), f32), pltpu.VMEM((levels, rows, cols), f32)
    vint = pltpu.VMEM((rows, cols), jnp.int32)
    flat = jax.ShapeDtypeStruct((FLAT_FIELDS, erows, ecols), f32)
    state = pl.pallas_call(
        functools.partial(kernel, rows * lax.axis_size("lat")),
        out_shape=(cube,) * 4 + (flat,),
        in_specs=[hbm] * 9,
        out_specs=(hbm,) * 5,
        scratch_shapes=(
            [vcube] * 4 + [vflat] + [pltpu.VMEM((levels, erows, ecols), f32)] * 4
            + [pltpu.VMEM((erows, ecols), f32)] * 3
            + [vcube]
            + [pltpu.VMEM((rows, LANES), f32)] * 2
            + [vplane] * 3 + [vint] * 2
            + buffers(send_rows) + buffers(flat_rows)
            + [pltpu.SemaphoreType.DMA((9,)), pltpu.SemaphoreType.DMA((4, rows // SUB))]
            + [pltpu.SemaphoreType.DMA((8,))] * 4
        ),
        compiler_params=pltpu.CompilerParams(
            collective_id=0, has_side_effects=True, vmem_limit_bytes=VMEM_BYTES),
    )(*args)
    return pl.pallas_call(
        closing,
        out_shape=(cube,) * 4 + (plane,) * 3,
        in_specs=[hbm] * 5,
        out_specs=(hbm,) * 7,
        scratch_shapes=(
            [vcube] * 4 + [vflat] + [vcube] * 2 + [vplane] * 3
            + [pltpu.VMEM((4, rows, cols), f32),
               pltpu.SemaphoreType.DMA((5,)),
               pltpu.SemaphoreType.DMA((5,)),
               pltpu.SemaphoreType.DMA((2, -(-levels // 4)))]
        ),
        compiler_params=pltpu.CompilerParams(vmem_limit_bytes=VMEM_BYTES),
    )(*state)


def solution(mesh):
    cube, plane = P(None, "lat", "lon"), P("lat", "lon")
    return jax.shard_map(
        body,
        mesh=mesh,
        in_specs=(cube,) * 4 + (plane,) * 5,
        out_specs=(cube,) * 4 + (plane,) * 3,
        check_vma=False,
    )
```

```python
import functools

import jax
import jax.numpy as jnp
from jax import lax
from jax.experimental import pallas as pl
from jax.experimental.pallas import tpu as pltpu
from jax.sharding import PartitionSpec as P

NSUB = 4
TIME_STEP = 0.4
TRACER_DIFF = 0.05
MOMENTUM_DIFF = 0.05
BOTTOM_DRAG = 0.05
WIND_FACTOR = 0.5
CORIOLIS_SCALE = 0.5
LATITUDE_SPAN = 2.6
GRAVITY_FACTOR = 0.3
THERMAL_COEF = 0.2
HALINE_COEF = 0.8
BACKGROUND_MIX = 0.05
CONVECTIVE_MIX = 1.5
STABILITY_FACTOR = 5.0
HEIGHT_FACTOR = 0.2
SLOPE_FACTOR = 0.15

LANES = 128
VMEM_BYTES = 67043328
SUB = 8
HALO_FIELDS = (2, 2, 1, 1)
HALO_DEPTH = 2
FLAT_HALO = NSUB
FLAT_FIELDS = 6
MESH = pl.DeviceIdType.MESH


def lane_shift(x, s):
    n = x.shape[-1]
    return pltpu.roll(x, (-s) % n, x.ndim - 1)


def row_shift(x, s):
    n = x.shape[0]
    return pltpu.roll(x, (-s) % n, 0)


def open_at(depth, k):
    return jnp.clip(depth - k, 0.0, 1.0)


def pack_strips(pieces, rows):
    lane = lax.broadcasted_iota(jnp.int32, (rows, LANES), 1)
    west = jnp.zeros((rows, LANES), jnp.float32)
    east = jnp.zeros((rows, LANES), jnp.float32)
    for first, last, width, at in pieces:
        mask = (lane >= at) & (lane < at + width)
        west = jnp.where(mask, pltpu.roll(first, at, 1) if at else first, west)
        east = jnp.where(mask, pltpu.roll(last, (at + width) % LANES, 1), east)
    return west, east


def halo_tile(from_east, from_west, width, at):
    lane = lax.broadcasted_iota(jnp.int32, from_east.shape, 1)
    return jnp.where(
        lane < LANES // 2,
        pltpu.roll(from_east, (-at) % LANES, 1),
        pltpu.roll(from_west, (-at - width) % LANES, 1),
    )


def kernel(
    lat_total,
    t_in, s_in, u_in, v_in, eta_hbm, zt_hbm, mt_hbm, wi_hbm, bi_hbm,
    t_hbm, s_hbm, u_hbm, v_hbm, flat_hbm,
    t_out, s_out, u_out, v_out, flat,
    te, se, ue, ve, de, hue, hve, ratio, fu_ref, fv_ref,
    eta_in, zt_in, mt_in, wi_in, bi_in,
    west1, east1, north1, south1, fe1, fw1, fn1, fs1,
    west2, east2, north2, south2, fe2, fw2, fn2, fs2,
    load_sem, store_sem, send1, recv1, send2, recv2,
):
    levels, rows, cols = t_out.shape
    lon, lat = lax.axis_index("lon"), lax.axis_index("lat")
    nlon, nlat = lax.axis_size("lon"), lax.axis_size("lat")
    wst, est = lax.rem(lon + nlon - 1, nlon), lax.rem(lon + 1, nlon)
    nth, sth = lax.rem(lat + 1, nlat), lax.rem(lat + nlat - 1, nlat)
    has_n, has_s = lat < nlat - 1, lat > 0
    top, bot = rows, SUB
    end = SUB + rows

    loads, stores = [], []

    def store_rows(n, src, dst, r):
        part = pl.ds(r, SUB)
        stores.append(pltpu.make_async_copy(src.at[:, part, :], dst.at[:, part, :], store_sem.at[n, r // SUB]))
        stores[-1].start()

    planes = ((wi_hbm, wi_in), (bi_hbm, bi_in), (eta_hbm, eta_in), (zt_hbm, zt_in), (mt_hbm, mt_in))
    cubes = ((t_in, te), (s_in, se), (u_in, ue), (v_in, ve))
    for n, (src, dst) in enumerate(planes):
        loads.append(pltpu.make_async_copy(src, dst, load_sem.at[n]))
    for n, (src, dst) in enumerate(cubes):
        loads.append(pltpu.make_async_copy(src, dst.at[:, SUB:end, 0:cols], load_sem.at[len(planes) + n]))
    for c in loads:
        c.start()

    barrier = pltpu.get_barrier_semaphore()

    def greet(lo, la):
        pl.semaphore_signal(barrier, inc=1, device_id=(lo, la), device_id_type=MESH)

    greet(wst, lat)
    greet(est, lat)

    @pl.when(has_n)
    def _():
        greet(wst, nth)
        greet(lon, nth)
        greet(est, nth)

    @pl.when(has_s)
    def _():
        greet(wst, sth)
        greet(lon, sth)
        greet(est, sth)

    def exchange(west, east, north, south, fe, fw, fn, fs, send, recv):
        def cp(n, src, dst, lo, la):
            return pltpu.make_async_remote_copy(
                src_ref=src, dst_ref=dst, send_sem=send.at[n], recv_sem=recv.at[n],
                device_id=(lo, la), device_id_type=MESH)

        lo_s, hi_s = pl.ds(0, SUB), pl.ds(rows - SUB, SUB)
        own, below, above = pl.ds(SUB, rows), pl.ds(0, SUB), pl.ds(end, SUB)
        along = [cp(0, west, fe.at[own], wst, lat), cp(1, east, fw.at[own], est, lat)]
        up = [cp(2, north, fs, lon, nth),
              cp(3, west.at[hi_s], fe.at[below], wst, nth),
              cp(4, east.at[hi_s], fw.at[below], est, nth)]
        down = [cp(5, south, fn, lon, sth),
                cp(6, west.at[lo_s], fe.at[above], wst, sth),
                cp(7, east.at[lo_s], fw.at[above], est, sth)]

        def start():
            @pl.when(has_n)
            def _():
                for c in up:
                    c.start()

            @pl.when(has_s)
            def _():
                for c in down:
                    c.start()

            for c in along:
                c.start()

        def finish_lon():
            for c in along:
                c.wait_recv()
                c.wait_send()

        def finish_lat():
            @pl.when(has_n)
            def _():
                for c in up:
                    c.wait_send()
                for c in down:
                    c.wait_recv()

            @pl.when(has_s)
            def _():
                for c in down:
                    c.wait_send()
                for c in up:
                    c.wait_recv()

        return start, finish_lon, finish_lat

    def clear_edges(fe, fw, fn, fs):
        @pl.when(jnp.logical_not(has_n))
        def _():
            fn[...] = jnp.zeros_like(fn)
            fe[end:, :] = jnp.zeros((SUB, LANES), jnp.float32)
            fw[end:, :] = jnp.zeros((SUB, LANES), jnp.float32)

        @pl.when(jnp.logical_not(has_s))
        def _():
            fs[...] = jnp.zeros_like(fs)
            fe[:SUB, :] = jnp.zeros((SUB, LANES), jnp.float32)
            fw[:SUB, :] = jnp.zeros((SUB, LANES), jnp.float32)

    clear_edges(fe1, fw1, fn1, fs1)
    clear_edges(fe2, fw2, fn2, fs2)
    row = lax.broadcasted_iota(jnp.int32, (rows, LANES), 0).astype(jnp.float32)
    row = row + (lat * rows).astype(jnp.float32)
    fu_ref[...] = CORIOLIS_SCALE * jnp.sin(LATITUDE_SPAN * ((row + 0.5) / lat_total - 0.5))
    fv_ref[...] = CORIOLIS_SCALE * jnp.sin(LATITUDE_SPAN * ((row + 1.0) / lat_total - 0.5))

    for c in loads:
        c.wait()
    depth = (wi_in[...] * bi_in[...]).astype(jnp.float32)
    de[SUB:end, 0:cols] = depth

    fields = (te, se, ue, ve)
    per_level = sum(HALO_FIELDS)
    depth_at = per_level * levels
    places = []
    for k in range(levels):
        at = per_level * k
        for ref, width in zip(fields, HALO_FIELDS):
            places.append((ref, k, width, at))
            at += width
    for ref, k, width, at in places:
        south1[at:at + width, :] = ref[k, SUB:SUB + width, 0:cols]
        north1[at:at + width, :] = ref[k, end - width:end, 0:cols]
    south1[depth_at:depth_at + HALO_DEPTH, :] = depth[:HALO_DEPTH]
    north1[depth_at:depth_at + HALO_DEPTH, :] = depth[rows - HALO_DEPTH:]
    pieces = [(ref[k, SUB:end, 0:LANES], ref[k, SUB:end, cols - LANES:cols], width, at)
              for ref, k, width, at in places]
    pieces.append((depth[:, :LANES], depth[:, cols - LANES:], HALO_DEPTH, depth_at))
    west, east = pack_strips(pieces, rows)
    west1[...] = west
    east1[...] = east

    pl.semaphore_wait(barrier, 2 + 3 * has_n.astype(jnp.int32) + 3 * has_s.astype(jnp.int32))

    start1, lon1, lat1 = exchange(west1, east1, north1, south1, fe1, fw1, fn1, fs1, send1, recv1)
    start1()

    def tracers(r):
        here = slice(SUB + r, 2 * SUB + r)
        out = slice(r, r + SUB)

        def at_rows(s):
            return slice(SUB + r + s, 2 * SUB + r + s)

        def star(k):
            kf = k.astype(jnp.float32) if hasattr(k, "astype") else jnp.float32(k)
            uw = ue[k, here, :]
            v0 = ve[k, here, 0:cols]
            v1 = ve[k, at_rows(-1), 0:cols]
            up, un = jnp.maximum(uw, 0.0) * (1.0 / 6.0), jnp.minimum(uw, 0.0) * (1.0 / 6.0)
            v0p, v0n = jnp.maximum(v0, 0.0) * (1.0 / 6.0), jnp.minimum(v0, 0.0) * (1.0 / 6.0)
            v1p, v1n = jnp.maximum(v1, 0.0) * (1.0 / 6.0), jnp.minimum(v1, 0.0) * (1.0 / 6.0)
            mu = TRACER_DIFF * open_at(hue[here, :], kf)
            m0 = TRACER_DIFF * open_at(hve[here, 0:cols], kf)
            m1 = TRACER_DIFF * open_at(hve[at_rows(-1), 0:cols], kf)
            res = []
            for ref in (te, se):
                c = ref[k, here, :]
                cw, ce, cee = lane_shift(c, -1), lane_shift(c, 1), lane_shift(c, 2)
                fx = up * (2.0 * c + 5.0 * ce - cee) + un * (5.0 * c + 2.0 * ce - cw) - mu * (ce - c)
                dx = fx[:, :cols] - lane_shift(fx, -1)[:, :cols]
                c0 = c[:, :cols]
                ss, s1 = ref[k, at_rows(-2), 0:cols], ref[k, at_rows(-1), 0:cols]
                n1, nn = ref[k, at_rows(1), 0:cols], ref[k, at_rows(2), 0:cols]
                f0 = v0p * (2.0 * c0 + 5.0 * n1 - nn) + v0n * (5.0 * c0 + 2.0 * n1 - s1) - m0 * (n1 - c0)
                f1 = v1p * (2.0 * s1 + 5.0 * c0 - n1) + v1n * (5.0 * s1 + 2.0 * c0 - ss) - m1 * (c0 - s1)
                res.append(c0 - TIME_STEP * (dx + f0 - f1))
            return res

        def eliminate(k, t, s, lower, upper, rat, pt, ps):
            inv = 1.0 / (1.0 + upper + lower * (1.0 - rat))
            pt = (t + lower * pt) * inv
            ps = (s + lower * ps) * inv
            rat = upper * inv
            t_out[k, out, :] = pt
            s_out[k, out, :] = ps
            ratio[k, out, :] = rat
            return rat, pt, ps

        def forward(k, carry):
            t, s, lower, rat, pt, ps = carry
            tn, sn = star(k)
            rise = jnp.maximum(HALINE_COEF * (sn - s) - THERMAL_COEF * (tn - t), 0.0)
            mix = BACKGROUND_MIX + CONVECTIVE_MIX / (1.0 + STABILITY_FACTOR * rise)
            upper = TIME_STEP * mix * open_at(de[here, 0:cols], k.astype(jnp.float32))
            rat, pt, ps = eliminate(k - 1, t, s, lower, upper, rat, pt, ps)
            return tn, sn, upper, rat, pt, ps

        zero = jnp.zeros((SUB, cols), jnp.float32)
        t, s = star(0)
        t, s, lower, rat, pt, ps = lax.fori_loop(1, levels, forward, (t, s, zero, zero, zero, zero))
        rat, pt, ps = eliminate(levels - 1, t, s, lower, zero, rat, pt, ps)

        def backward(i, carry):
            t, s = carry
            k = levels - 2 - i
            rat = ratio[k, out, :]
            t = t_out[k, out, :] + rat * t
            s = s_out[k, out, :] + rat * s
            t_out[k, out, :] = t
            s_out[k, out, :] = s
            return t, s

        lax.fori_loop(0, levels - 1, backward, (pt, ps))
        store_rows(2, t_out, t_hbm, r)
        store_rows(3, s_out, s_hbm, r)

    lon1()
    own, last = slice(SUB, end), rows
    fe, fw = fe1[own, :], fw1[own, :]
    for ref, k, width, at in places:
        ref[k, own, cols:] = halo_tile(fe, fw, width, at)
    de[own, cols:] = halo_tile(fe, fw, HALO_DEPTH, depth_at)
    d = de[own, :]
    hue[own, :] = jnp.minimum(d, lane_shift(d, 1))
    hve[own, :] = jnp.minimum(d, row_shift(d, 1))

    @pl.loop(0, levels)
    def _(k):
        kf = k.astype(jnp.float32)
        wet = open_at(de[own, :], kf)
        te[k, own, :] = te[k, own, :] * wet
        se[k, own, :] = se[k, own, :] * wet
        ue[k, own, :] = ue[k, own, :] * open_at(hue[own, :], kf)
        ve[k, SUB:last, :] = ve[k, SUB:last, :] * open_at(hve[SUB:last, :], kf)

    for r in range(SUB, rows - SUB, SUB):
        tracers(r)

    lat1()
    edges = (slice(0, SUB), slice(end, end + SUB))
    for rim in edges:
        fe, fw = fe1[rim, :], fw1[rim, :]
        for ref, k, width, at in places:
            if width == 1:
                ref[k, rim, cols:] = halo_tile(fe, fw, width, at)
        de[rim, cols:] = halo_tile(fe, fw, HALO_DEPTH, depth_at)
    for ref, k, width, at in places:
        ref[k, SUB - width:SUB, 0:cols] = fs1[at:at + width, :]
        ref[k, end:end + width, 0:cols] = fn1[at:at + width, :]
    de[SUB - HALO_DEPTH:SUB, 0:cols] = fs1[depth_at:depth_at + HALO_DEPTH, :]
    de[end:end + HALO_DEPTH, 0:cols] = fn1[depth_at:depth_at + HALO_DEPTH, :]
    d = de[...]
    hue[...] = jnp.minimum(d, lane_shift(d, 1))
    hve[...] = jnp.minimum(d, row_shift(d, 1))

    @pl.loop(0, levels)
    def _(k):
        kf = k.astype(jnp.float32)
        for rim in edges:
            wet = open_at(de[rim, :], kf)
            te[k, rim, :] = te[k, rim, :] * wet
            se[k, rim, :] = se[k, rim, :] * wet
            ue[k, rim, :] = ue[k, rim, :] * open_at(hue[rim, :], kf)
        for rim in (slice(0, SUB), slice(last, end + SUB)):
            ve[k, rim, :] = ve[k, rim, :] * open_at(hve[rim, :], kf)

    for r in range(0, rows, SUB):
        here = slice(SUB + r, 2 * SUB + r)
        above = slice(SUB + r + 1, 2 * SUB + r + 1)
        below = slice(SUB + r - 1, 2 * SUB + r - 1)
        out = slice(r, r + SUB)
        fu = jnp.broadcast_to(fu_ref[out, 0:1], (SUB, cols))
        fv = jnp.broadcast_to(fv_ref[out, 0:1], (SUB, cols))

        def momentum(k, carry):
            cgx, cgy, su, sv, gu, gv = carry
            kf = k.astype(jnp.float32)
            wind = jnp.where(k == 0, TIME_STEP * WIND_FACTOR, 0.0)
            uw, un, us = ue[k, here, :], ue[k, above, :], ue[k, below, 0:cols]
            vw, vn, vs = ve[k, here, :], ve[k, above, 0:cols], ve[k, below, :]
            u, v = uw[:, :cols], vw[:, :cols]
            a = vw + vs
            b = uw + un
            v_at_u = 0.25 * (a[:, :cols] + lane_shift(a, 1)[:, :cols])
            u_at_v = 0.25 * (b[:, :cols] + lane_shift(b, -1)[:, :cols])
            lap_u = lane_shift(uw, 1)[:, :cols] + lane_shift(uw, -1)[:, :cols] + un[:, :cols] + us - 4.0 * u
            lap_v = lane_shift(vw, 1)[:, :cols] + lane_shift(vw, -1)[:, :cols] + vn + vs[:, :cols] - 4.0 * v
            rho = HALINE_COEF * se[k, here, :] - THERMAL_COEF * te[k, here, :]
            rho_n = HALINE_COEF * se[k, above, 0:cols] - THERMAL_COEF * te[k, above, 0:cols]
            gx = lane_shift(rho, 1)[:, :cols] - rho[:, :cols]
            gy = rho_n - rho[:, :cols]
            cgx = cgx + gx
            cgy = cgy + gy
            px = GRAVITY_FACTOR * (cgx - 0.5 * gx)
            py = GRAVITY_FACTOR * (cgy - 0.5 * gy)
            mu = open_at(hue[here, 0:cols], kf)
            mv = open_at(hve[here, 0:cols], kf)
            ut = mu * (u + TIME_STEP * (fu * v_at_u - px + MOMENTUM_DIFF * lap_u - BOTTOM_DRAG * u)
                       + wind * zt_in[out, :])
            vt = mv * (v + TIME_STEP * (-fv * u_at_v - py + MOMENTUM_DIFF * lap_v - BOTTOM_DRAG * v)
                       + wind * mt_in[out, :])
            u_out[k, out, :] = ut
            v_out[k, out, :] = vt
            return cgx, cgy, su + u, sv + v, gu + (ut - u), gv + (vt - v)

        zero = jnp.zeros((SUB, cols), jnp.float32)
        _, _, su, sv, gu, gv = lax.fori_loop(0, levels, momentum, (zero,) * 6)
        store_rows(0, u_out, u_hbm, r)
        store_rows(1, v_out, v_hbm, r)
        flat[0, here, 0:cols] = eta_in[out, :]
        flat[1, here, 0:cols] = su
        flat[2, here, 0:cols] = sv
        flat[3, here, 0:cols] = gu
        flat[4, here, 0:cols] = gv
        flat[5, here, 0:cols] = de[here, 0:cols]

    pieces = []
    for f in range(FLAT_FIELDS):
        at = FLAT_HALO * f
        south2[at:at + FLAT_HALO, :] = flat[f, SUB:SUB + FLAT_HALO, 0:cols]
        north2[at:at + FLAT_HALO, :] = flat[f, end - FLAT_HALO:end, 0:cols]
        pieces.append((flat[f, SUB:end, 0:LANES], flat[f, SUB:end, cols - LANES:cols], FLAT_HALO, at))
    west, east = pack_strips(pieces, rows)
    west2[...] = west
    east2[...] = east
    start2, lon2, lat2 = exchange(west2, east2, north2, south2, fe2, fw2, fn2, fs2, send2, recv2)
    start2()

    for r in sorted({0, rows - SUB}):
        tracers(r)

    lon2()
    lat2()

    fe, fw = fe2[...], fw2[...]
    for f in range(FLAT_FIELDS):
        at = FLAT_HALO * f
        flat[f, :, cols:] = halo_tile(fe, fw, FLAT_HALO, at)
        flat[f, SUB - FLAT_HALO:SUB, 0:cols] = fs2[at:at + FLAT_HALO, :]
        flat[f, end:end + FLAT_HALO, 0:cols] = fn2[at:at + FLAT_HALO, :]
    stores.append(pltpu.make_async_copy(flat, flat_hbm, load_sem.at[0]))
    stores[-1].start()
    for c in stores:
        c.wait()


def closing(
    t_old, s_old, u_old, v_old, flat_old,
    t_hbm, s_hbm, u_hbm, v_hbm, eta_hbm, tx_hbm, ty_hbm,
    t_in, s_in, u_in, v_in, flat,
    u_next, v_next, eta_out, tx_out, ty_out, corr, load_sem, sem, level_sem,
):
    levels, rows, cols = t_in.shape
    end = SUB + rows
    loads = []
    for n, (src, dst) in enumerate(
        ((flat_old, flat), (t_old, t_in), (s_old, s_in), (u_old, u_in), (v_old, v_in))
    ):
        loads.append(pltpu.make_async_copy(src, dst, load_sem.at[n]))
        loads[-1].start()
    stores = []
    loads[0].wait()

    eta, bu, bv = flat[0], flat[1], flat[2]
    su, sv = bu[SUB:end, :cols], bv[SUB:end, :cols]
    gu, gv, d = flat[3], flat[4], flat[5]
    hu = jnp.minimum(d, lane_shift(d, 1))
    hv = jnp.minimum(d, row_shift(d, 1))
    mouth_u, mouth_v = jnp.minimum(hu, 1.0), jnp.minimum(hv, 1.0)
    for _ in range(NSUB):
        eta = eta - HEIGHT_FACTOR * (bu - lane_shift(bu, -1) + bv - row_shift(bv, -1))
        bu = mouth_u * (bu + gu / NSUB - SLOPE_FACTOR * hu * (lane_shift(eta, 1) - eta))
        bv = mouth_v * (bv + gv / NSUB - SLOPE_FACTOR * hv * (row_shift(eta, 1) - eta))
    loads[1].wait()
    loads[2].wait()
    for n, (src, dst) in enumerate(((t_in, t_hbm), (s_in, s_hbm))):
        stores.append(pltpu.make_async_copy(src, dst, sem.at[n]))
        stores[-1].start()
    eta_out[...] = eta[SUB:end, :cols]
    tu, tv = bu[SUB:end, :cols], bv[SUB:end, :cols]
    tx_out[...] = tu
    ty_out[...] = tv
    for n, (src, dst) in enumerate(((eta_out, eta_hbm), (tx_out, tx_hbm), (ty_out, ty_hbm))):
        stores.append(pltpu.make_async_copy(src, dst, sem.at[2 + n]))
        stores[-1].start()
    hu, hv = hu[SUB:end, :cols], hv[SUB:end, :cols]
    corr[0] = (tu - (gu[SUB:end, :cols] + su)) / jnp.maximum(hu, 1.0)
    corr[1] = (tv - (gv[SUB:end, :cols] + sv)) / jnp.maximum(hv, 1.0)
    corr[2] = hu
    corr[3] = hv
    loads[3].wait()
    loads[4].wait()

    for k in range(levels):
        u_next[k] = open_at(corr[2], float(k)) * (u_in[k] + corr[0])
        v_next[k] = open_at(corr[3], float(k)) * (v_in[k] + corr[1])
        if k % 4 == 3 or k == levels - 1:
            part = pl.ds(k - k % 4, k % 4 + 1)
            for n, (src, dst) in enumerate(((u_next, u_hbm), (v_next, v_hbm))):
                stores.append(pltpu.make_async_copy(src.at[part], dst.at[part], level_sem.at[n, k // 4]))
                stores[-1].start()
    for c in stores:
        c.wait()


def body(*args):
    levels, rows, cols = args[0].shape
    f32 = jnp.float32
    cube = jax.ShapeDtypeStruct((levels, rows, cols), f32)
    plane = jax.ShapeDtypeStruct((rows, cols), f32)
    erows, ecols = rows + 2 * SUB, cols + LANES
    send_rows = -(-(sum(HALO_FIELDS) * levels + HALO_DEPTH) // SUB) * SUB
    flat_rows = FLAT_FIELDS * FLAT_HALO

    def buffers(n):
        strip, ext = pltpu.VMEM((rows, LANES), f32), pltpu.VMEM((erows, LANES), f32)
        block = pltpu.VMEM((n, cols), f32)
        return [strip, strip, block, block, ext, ext, block, block]

    vflat = pltpu.VMEM((FLAT_FIELDS, erows, ecols), f32)
    hbm = pl.BlockSpec(memory_space=pltpu.HBM)
    vplane, vcube = pltpu.VMEM((rows, cols), f32), pltpu.VMEM((levels, rows, cols), f32)
    vint = pltpu.VMEM((rows, cols), jnp.int32)
    flat = jax.ShapeDtypeStruct((FLAT_FIELDS, erows, ecols), f32)
    state = pl.pallas_call(
        functools.partial(kernel, rows * lax.axis_size("lat")),
        out_shape=(cube,) * 4 + (flat,),
        in_specs=[hbm] * 9,
        out_specs=(hbm,) * 5,
        scratch_shapes=(
            [vcube] * 4 + [vflat] + [pltpu.VMEM((levels, erows, ecols), f32)] * 4
            + [pltpu.VMEM((erows, ecols), f32)] * 3
            + [vcube]
            + [pltpu.VMEM((rows, LANES), f32)] * 2
            + [vplane] * 3 + [vint] * 2
            + buffers(send_rows) + buffers(flat_rows)
            + [pltpu.SemaphoreType.DMA((9,)), pltpu.SemaphoreType.DMA((4, rows // SUB))]
            + [pltpu.SemaphoreType.DMA((8,))] * 4
        ),
        compiler_params=pltpu.CompilerParams(
            collective_id=0, has_side_effects=True, vmem_limit_bytes=VMEM_BYTES),
    )(*args)
    return pl.pallas_call(
        closing,
        out_shape=(cube,) * 4 + (plane,) * 3,
        in_specs=[hbm] * 5,
        out_specs=(hbm,) * 7,
        scratch_shapes=(
            [vcube] * 4 + [vflat] + [vcube] * 2 + [vplane] * 3
            + [pltpu.VMEM((4, rows, cols), f32),
               pltpu.SemaphoreType.DMA((5,)),
               pltpu.SemaphoreType.DMA((5,)),
               pltpu.SemaphoreType.DMA((2, -(-levels // 4)))]
        ),
        compiler_params=pltpu.CompilerParams(vmem_limit_bytes=VMEM_BYTES),
    )(*state)


def solution(mesh):
    cube, plane = P(None, "lat", "lon"), P("lat", "lon")
    return jax.shard_map(
        body,
        mesh=mesh,
        in_specs=(cube,) * 4 + (plane,) * 5,
        out_specs=(cube,) * 4 + (plane,) * 3,
        check_vma=False,
    )
```
